32 devices in a mesh: clus: 4 (over y, x), fsdp: 4 (over z), head: 2 (over core).
Axes of the slice: x: 2, y: 2, z: 4, core: 2. Of those that a mesh axis runs over, the one named last changes fastest.
Arguments:
- feats: bfloat16 [4096, 2048], P(('clus', 'fsdp')), as said below
- w_query: float32 [2048, 2048], P(('clus', 'fsdp'), 'head'), may hold values from -0.125 to 0.125
- w_keyval: float32 [2048, 2048], P(('clus', 'fsdp'), 'head'), may hold values from -0.125 to 0.125
- grad_out: bfloat16 [4096, 2048], P(('clus', 'fsdp'), 'head'), may hold values from -6 to 6
- col_block: int32 [32, 5], replicated, may hold values from 0 to 31, as said below
- col_count: int32 [32], replicated, may hold values from 4 to 5
Outputs:
- out: bfloat16 [4096, 2048], P(('clus', 'fsdp'), 'head')
- grad_w_query: float32 [2048, 2048], P(('clus', 'fsdp'), 'head')
- grad_w_keyval: float32 [2048, 2048], P(('clus', 'fsdp'), 'head')
The draws below stay inside these ranges and needn't reach their ends.
Inputs may be any that keep to these rules, and one draw needn't show every extreme that they name: `col_block`: column 0 of row b is b itself; column 1 is another block of b's cluster (cluster of a block = block // 2); the other columns lie in other clusters whose index differs from b's cluster by a nonzero multiple of 4. A row names each block at most once. The rows of one cluster name, in any other cluster, at most one distinct block. `feats`: node features of order one, rows of differing scale.
All inputs are finite; a program needn't handle non-finite values.
Results may differ from the reference program's by a relative error of at most 0.014.
The reference program's roundings to bfloat16 on the way (of `wq`, `wkv`, `query`, `keyval`, `prob_b`, `dscore`, `dquery` and `dkeyval`) count: a program that leaves them out, or rounds other values in their place, can miss the bound.
Values may be sent and summed in bfloat16 or wider, within the bound.
No kernel may reach another device: no remote copies, remote signals or barrier semaphores. Data moves between devices by JAX's collectives and lax.ppermute only.
A program may use at most 128 MiB of HBM per device.

```python
import math
import jax
import jax.numpy as jnp
from jax import lax

D = 2048
HEADS = 16
HD = 128
BLK = 128
NB_DEV = 2
NCOL = 5
CLUSTERS = 16
NBLK = 32
NODES = 4096
N_CLUS = 4
N_FSDP = 4


def draw_feats(key, part):
    first, second = jax.random.split(key, 2)
    base = jax.random.normal(first, (NODES, D), jnp.float32)
    scales = jnp.exp(jax.random.uniform(second, (NODES, 1), jnp.float32, 0.0, math.log(3.0)))
    return (base * scales).astype(jnp.bfloat16)


def draw_col_block(key, part):
    first, second, third = jax.random.split(key, 3)
    cluster_ids = jnp.arange(CLUSTERS, dtype=jnp.int32)
    clus_index = cluster_ids // N_FSDP
    fsdp_index = cluster_ids % N_FSDP
    local = jnp.arange(NB_DEV, dtype=jnp.int32)
    base = cluster_ids[:, None] * NB_DEV
    own = base + local[None, :]
    offset = jax.random.randint(first, (CLUSTERS, NB_DEV), 1, NB_DEV, dtype=jnp.int32)
    other = base + (local[None, :] + offset) % NB_DEV
    cluster_keys = jax.random.split(second, CLUSTERS)

    def peer_order(one_key):
        return jax.random.permutation(one_key, N_CLUS - 1).astype(jnp.int32)
    orders = jax.vmap(peer_order)(cluster_keys)
    source = jax.random.randint(third, (CLUSTERS, N_CLUS), 0, NB_DEV, dtype=jnp.int32)
    columns = [own, other]
    for column in range(NCOL - 2):
        position = (local * (NCOL - 2) + column) % (N_CLUS - 1)
        shifts = jnp.take(orders, position, axis=1)
        peers = (clus_index[:, None] + 1 + shifts) % N_CLUS
        chosen = jnp.take_along_axis(source, peers, axis=1)
        target = peers * N_FSDP + fsdp_index[:, None]
        columns.append(target * NB_DEV + chosen)
    return jnp.stack(columns, -1).reshape(NBLK, NCOL).astype(jnp.int32)


def place_ends(array, rng, low, top_value):
    extent = array.shape
    spot = [jax.random.randint(jax.random.fold_in(rng, axis), (), 0, extent[axis]) for axis in range(len(extent))]
    array = array.at[tuple(spot)].set(low)
    longest = extent.index(max(extent))
    spot[longest] = (spot[longest] + 1) % extent[longest]
    return array.at[tuple(spot)].set(top_value)


def shard_levels(stream_key, extent, pieces, least, top_value):
    factor_of = 1.0
    for dim, blocks in pieces:
        steps = jax.random.uniform(jax.random.fold_in(jax.random.fold_in(stream_key, 6), dim), (blocks,), jnp.float32, least / len(pieces), top_value / len(pieces))
        factor_of = factor_of * jnp.repeat(jnp.exp(steps), extent[dim] // blocks).reshape((-1,) + (1,) * (len(extent) - 1 - dim))
    return factor_of


def scatter_about(key, extent, width, reach, shards=(), kind=jnp.bfloat16):
    entries = width * jax.random.normal(key, extent, jnp.float32)
    if shards:
        entries = entries * shard_levels(key, extent, shards, -0.22, 0.18)
    return jnp.clip(entries, -reach, reach).astype(kind)


def setup_inputs(seed: int = 0) -> dict:
    seeds = jax.random.split(jax.random.key(seed), 7)
    feats = draw_feats(jax.random.fold_in(seeds[6], 71), 0)
    w_query = scatter_about(seeds[1], (D, D), D ** -0.5, 0.125, ((0, 16), (1, 2)), jnp.float32)
    w_keyval = scatter_about(seeds[2], (D, D), D ** -0.5, 0.125, ((0, 16), (1, 2)), jnp.float32)
    grad_out = scatter_about(seeds[3], (NODES, D), 1.0, 6.0, ((0, 16), (1, 2)))
    col_block = draw_col_block(jax.random.fold_in(seeds[6], 71), 0)
    col_count = place_ends(jax.random.randint(seeds[5], (NBLK,), NCOL - 1, NCOL + 1), jax.random.fold_in(seeds[5], 1), NCOL - 1, NCOL).astype(jnp.int32)
    return {"feats": feats, "w_query": w_query, "w_keyval": w_keyval, "grad_out": grad_out, "col_block": col_block, "col_count": col_count}


def reference(feats, w_query, w_keyval, grad_out, col_block, col_count):
    wq = w_query.astype(jnp.bfloat16)
    wkv = w_keyval.astype(jnp.bfloat16)
    query = jnp.dot(feats, wq, preferred_element_type=jnp.float32).astype(jnp.bfloat16)
    keyval = jnp.dot(feats, wkv, preferred_element_type=jnp.float32).astype(jnp.bfloat16)
    scale = 1.0 / math.sqrt(HD)
    panels = keyval.reshape(NBLK, BLK, HEADS, HD)
    queries = query.reshape(NBLK, BLK, HEADS, HD)
    cotans = grad_out.reshape(NBLK, BLK, HEADS, HD)

    def one_block(carry, index):
        cols = col_block[index]
        count = col_count[index]
        keys = panels[cols].reshape(NCOL * BLK, HEADS, HD).astype(jnp.float32)
        qblock = queries[index].astype(jnp.float32)
        gblock = cotans[index].astype(jnp.float32)
        valid = jnp.repeat(jnp.arange(NCOL, dtype=jnp.int32) < count, BLK)
        score = jnp.einsum('qhd,khd->hqk', qblock, keys) * scale
        score = jnp.where(valid[None, None, :], score, -1e+30)
        top = lax.optimization_barrier(jnp.max(score, axis=-1, keepdims=True))
        expo = jnp.exp(score - top)
        prob = expo / lax.optimization_barrier(jnp.sum(expo, axis=-1, keepdims=True))
        prob_b = prob.astype(jnp.bfloat16).astype(jnp.float32)
        out_block = jnp.einsum('hqk,khd->qhd', prob_b, keys).astype(jnp.bfloat16)
        dprob = jnp.einsum('qhd,khd->hqk', gblock, keys)
        delta = lax.optimization_barrier(jnp.sum(prob * dprob, axis=-1, keepdims=True))
        dscore = (prob * (dprob - delta)).astype(jnp.bfloat16).astype(jnp.float32)
        dquery = (jnp.einsum('hqk,khd->qhd', dscore, keys) * scale).astype(jnp.bfloat16)
        dkeys = jnp.einsum('hqk,qhd->khd', dscore, qblock) * scale + jnp.einsum('hqk,qhd->khd', prob_b, gblock)
        carry = carry.at[cols].add(dkeys.reshape(NCOL, BLK, HEADS, HD))
        return (carry, (out_block, dquery))
    start = jnp.zeros((NBLK, BLK, HEADS, HD), jnp.float32)
    totals, (out_blocks, dquery_blocks) = lax.scan(one_block, start, jnp.arange(NBLK, dtype=jnp.int32))
    out = out_blocks.reshape(NODES, D)
    dquery = dquery_blocks.reshape(NODES, D)
    dkeyval = totals.reshape(NODES, D).astype(jnp.bfloat16)
    rows_group = NB_DEV * BLK

    def add_group(carry, group):
        first = (group * rows_group).astype(jnp.int32)
        block_feats = lax.dynamic_slice_in_dim(feats, first, rows_group, 0)
        block_dq = lax.dynamic_slice_in_dim(dquery, first, rows_group, 0)
        block_dk = lax.dynamic_slice_in_dim(dkeyval, first, rows_group, 0)
        dims = (((0,), (0,)), ((), ()))
        term_q = lax.dot_general(block_feats, block_dq, dims, preferred_element_type=jnp.float32)
        term_k = lax.dot_general(block_feats, block_dk, dims, preferred_element_type=jnp.float32)
        term_q = lax.optimization_barrier(term_q.astype(jnp.bfloat16)).astype(jnp.float32)
        term_k = lax.optimization_barrier(term_k.astype(jnp.bfloat16)).astype(jnp.float32)
        return ((carry[0] + term_q, carry[1] + term_k), None)
    zeros = jnp.zeros((D, D), jnp.float32)
    (grad_q, grad_k), _ = lax.scan(add_group, (zeros, zeros), jnp.arange(CLUSTERS, dtype=jnp.int32))
    return (out, grad_q, grad_k)
```

```python
import math

import jax
import jax.numpy as jnp
from jax import lax
from jax.experimental import pallas as pl
from jax.experimental.pallas import tpu as pltpu
from jax.sharding import PartitionSpec as P

HD = 128
BLK = 128
NCOL = 5

ANY = pl.BlockSpec(memory_space=pl.ANY)
SMEM = pl.BlockSpec(memory_space=pltpu.SMEM)
VMEM = pl.BlockSpec(memory_space=pltpu.VMEM)


def split_weights(wq_ref, wkv_ref, *out_refs):
    slots = len(out_refs)
    for j, out_ref in enumerate(out_refs):
        for d in range(out_ref.shape[0]):
            at = (d * slots + j) * HD
            out_ref[d, :, :HD] = wq_ref[:, at : at + HD].astype(jnp.bfloat16)
            out_ref[d, :, HD:] = wkv_ref[:, at : at + HD].astype(jnp.bfloat16)


def split_heads(x_ref, *out_refs):
    slots = len(out_refs)
    for j, out_ref in enumerate(out_refs):
        for d in range(out_ref.shape[0]):
            at = (d * slots + j) * HD
            out_ref[d] = x_ref[:, at : at + HD]


def merge_heads(*refs):
    *in_refs, out_ref = refs
    slots = len(in_refs)
    for j, in_ref in enumerate(in_refs):
        for d in range(in_ref.shape[0]):
            at = (d * slots + j) * HD
            out_ref[:, at : at + HD] = in_ref[d]


def merge_grads(*refs):
    *in_refs, gq_ref, gkv_ref = refs
    slots = len(in_refs)
    for j, in_ref in enumerate(in_refs):
        for d in range(in_ref.shape[0]):
            at = (d * slots + j) * HD
            gq_ref[:, at : at + HD] = in_ref[d, :HD, :].astype(jnp.float32).T
            gkv_ref[:, at : at + HD] = in_ref[d, HD:, :].astype(jnp.float32).T


def head_kernel(
    pos_ref,
    cols_ref,
    counts_ref,
    feats_ref,
    mine1_ref,
    mine2_ref,
    mine3_ref,
    other1_ref,
    other2_ref,
    other3_ref,
    w0_ref,
    wup_ref,
    wdn_ref,
    wfar_up_ref,
    wfar_dn_ref,
    cotan_ref,
    out_ref,
    grad0_ref,
    grad1_ref,
    grad2_ref,
    grad3_ref,
    f_ref,
    w_ref,
    g_ref,
    qkv_ref,
    dkv_ref,
    dqkv_ref,
    grad_ref,
    sems,
    out_sems,
):
    clus_at = pos_ref[0]
    fsdp_at = pos_ref[1]
    head_at = pos_ref[2]
    rows, width = feats_ref.shape
    half = width // 2
    nodes = f_ref.shape[0]
    scale = 1.0 / math.sqrt(HD)
    feat_copies = [
        pltpu.make_async_copy(feats_ref, f_ref.at[pl.ds(pl.multiple_of(clus_at * rows, rows), rows), :], sems.at[0])
    ]
    for m, (mine, other) in enumerate(
        ((mine1_ref, other1_ref), (mine2_ref, other2_ref), (mine3_ref, other3_ref)), 1
    ):
        at = pl.ds(pl.multiple_of((clus_at ^ m) * rows, rows), rows)
        feat_copies.append(
            pltpu.make_async_copy(
                mine, f_ref.at[at, pl.ds(pl.multiple_of(head_at * half, half), half)], sems.at[m]
            )
        )
        feat_copies.append(
            pltpu.make_async_copy(
                other, f_ref.at[at, pl.ds(pl.multiple_of((1 - head_at) * half, half), half)], sems.at[m + 3]
            )
        )
    near = [
        pltpu.make_async_copy(w0_ref, w_ref.at[:, fsdp_at], sems.at[7]),
        pltpu.make_async_copy(wup_ref, w_ref.at[:, (fsdp_at + 3) % 4], sems.at[8]),
        pltpu.make_async_copy(wdn_ref, w_ref.at[:, (fsdp_at + 1) % 4], sems.at[9]),
        pltpu.make_async_copy(cotan_ref, g_ref, sems.at[11]),
    ]
    far_up = pltpu.make_async_copy(wfar_up_ref, w_ref.at[:, (fsdp_at + 2) % 4], sems.at[10])
    far_dn = pltpu.make_async_copy(wfar_dn_ref, w_ref.at[:, (fsdp_at + 2) % 4], sems.at[10])
    for copy in feat_copies + near:
        copy.start()

    @pl.when(fsdp_at >= 2)
    def _():
        far_up.start()
        far_up.wait()

    @pl.when(fsdp_at < 2)
    def _():
        far_dn.start()
        far_dn.wait()

    dkv_ref[...] = jnp.zeros_like(dkv_ref)
    for copy in feat_copies + near:
        copy.wait()
    weights = w_ref[...].reshape(width, 2 * HD)
    for r in range(nodes // rows):
        at = slice(r * rows, (r + 1) * rows)
        qkv_ref[at, :] = jnp.dot(f_ref[at, :], weights, preferred_element_type=jnp.float32).astype(
            jnp.bfloat16
        )
    nt = (((1,), (1,)), ((), ()))
    tn = (((0,), (0,)), ((), ()))
    place = lax.broadcasted_iota(jnp.int32, (BLK, NCOL * BLK), 1)
    for b in range(nodes // BLK):
        at = slice(b * BLK, (b + 1) * BLK)
        query = qkv_ref[at, :HD]
        cotan = g_ref[at, :]
        listed = [pl.ds(pl.multiple_of(cols_ref[b, n] * BLK, BLK), BLK) for n in range(NCOL)]
        keys = jnp.concatenate([qkv_ref[rows_at, HD:] for rows_at in listed], 0)
        score = lax.dot_general(query, keys, nt, preferred_element_type=jnp.float32) * scale
        score = jnp.where(place < counts_ref[b] * BLK, score, -1e30)
        top = jnp.max(score, axis=-1, keepdims=True)
        expo = jnp.exp(score - top)
        prob = expo / jnp.sum(expo, axis=-1, keepdims=True)
        prob_b = prob.astype(jnp.bfloat16)
        out_ref[at, :] = jnp.dot(prob_b, keys, preferred_element_type=jnp.float32).astype(jnp.bfloat16)
        dprob = lax.dot_general(cotan, keys, nt, preferred_element_type=jnp.float32)
        delta = jnp.sum(prob * dprob, axis=-1, keepdims=True)
        dscore = (prob * (dprob - delta)).astype(jnp.bfloat16)
        dqkv_ref[at, :HD] = (
            jnp.dot(dscore, keys, preferred_element_type=jnp.float32) * scale
        ).astype(jnp.bfloat16)
        dkeys = lax.dot_general(dscore, query, tn, preferred_element_type=jnp.float32) * scale
        dkeys = dkeys + lax.dot_general(prob_b, cotan, tn, preferred_element_type=jnp.float32)
        for n, rows_at in enumerate(listed):
            dkv_ref[rows_at, :] = dkv_ref[rows_at, :] + dkeys[n * BLK : (n + 1) * BLK]
    dqkv_ref[:, HD:] = dkv_ref[...].astype(jnp.bfloat16)
    planes, owners = grad_ref.shape[:2]
    step = width // owners
    part = step // planes
    for s in range(owners):
        term = lax.dot_general(
            dqkv_ref[...], f_ref[:, s * step : (s + 1) * step], tn, preferred_element_type=jnp.float32
        ).astype(jnp.bfloat16)
        for f in range(planes):
            grad_ref[f, s] = term[:, f * part : (f + 1) * part]
    copies = [
        pltpu.make_async_copy(grad_ref.at[(fsdp_at + k) % 4], ref, out_sems.at[k])
        for k, ref in enumerate((grad0_ref, grad1_ref, grad2_ref, grad3_ref))
    ]
    for copy in copies:
        copy.start()
    for copy in copies:
        copy.wait()


def in_plane(feats, w_query, w_keyval, grad_out, col_block, col_count):
    rows, width = feats.shape
    wrows, half = w_query.shape
    nlocal = rows // BLK
    nclus = lax.axis_size("clus")
    nfsdp = lax.axis_size("fsdp")
    slots = half // HD // nclus
    clus_at = lax.axis_index("clus")
    fsdp_at = lax.axis_index("fsdp")
    head_at = lax.axis_index("head")
    nodes = nclus * rows
    bf16 = jnp.bfloat16

    def shape(dims, dtype=bf16):
        return jax.ShapeDtypeStruct(dims, dtype)

    def shift(x, pairs):
        return lax.ppermute(x, "fsdp", pairs)

    up_ring = [(i, (i + 1) % nfsdp) for i in range(nfsdp)]
    dn_ring = [(i, (i - 1) % nfsdp) for i in range(nfsdp)]
    parts = pl.pallas_call(
        split_weights,
        in_specs=[VMEM] * 2,
        out_specs=[VMEM] * slots,
        out_shape=[shape((nclus, wrows, 2 * HD))] * slots,
        name="split_weights",
    )(w_query, w_keyval)
    own_w = [lax.all_to_all(x, "clus", 0, 0, tiled=True) for x in parts]
    mine = lax.dynamic_slice_in_dim(feats, head_at * (width // 2), width // 2, 1)
    near = [lax.ppermute(mine, "clus", [(i, i ^ m) for i in range(nclus)]) for m in (1, 2, 3)]
    far = [lax.ppermute(x, "head", [(0, 1), (1, 0)]) for x in near]
    cotans = pl.pallas_call(
        split_heads,
        in_specs=[VMEM],
        out_specs=[VMEM] * slots,
        out_shape=[shape((nclus, rows, HD))] * slots,
        name="split_cotans",
    )(grad_out)
    cotans = [lax.all_to_all(x, "clus", 0, 0, tiled=True).reshape(nodes, HD) for x in cotans]
    all_cols = col_block.reshape(nclus, nfsdp, nlocal, NCOL)
    cols = lax.dynamic_index_in_dim(all_cols, fsdp_at, 1, keepdims=False).reshape(nclus * nlocal, NCOL)
    cols = cols // nlocal // nfsdp * nlocal + cols % nlocal
    counts = lax.dynamic_index_in_dim(
        col_count.reshape(nclus, nfsdp, nlocal), fsdp_at, 1, keepdims=False
    ).reshape(nclus * nlocal)
    pos = jnp.stack([clus_at, fsdp_at, head_at]).astype(jnp.int32)
    outs = []
    grads = []
    piece = (nclus, 2 * HD, wrows)
    for j in range(slots):
        w0 = own_w[j]
        wup = shift(w0, up_ring)
        wdn = shift(w0, dn_ring)
        wfar_up = shift(wup, [(1, 2), (2, 3)])
        wfar_dn = shift(wdn, [(2, 1), (1, 0)])
        out, g0, g1, g2, g3 = pl.pallas_call(
            head_kernel,
            in_specs=[SMEM] * 3 + [ANY] * 13,
            out_specs=[VMEM] + [ANY] * 4,
            out_shape=[shape((nodes, HD))] + [shape(piece)] * 4,
            scratch_shapes=[
                pltpu.VMEM((nodes, width), bf16),
                pltpu.VMEM((nclus, nfsdp, wrows, 2 * HD), bf16),
                pltpu.VMEM((nodes, HD), bf16),
                pltpu.VMEM((nodes, 2 * HD), bf16),
                pltpu.VMEM((nodes, HD), jnp.float32),
                pltpu.VMEM((nodes, 2 * HD), bf16),
                pltpu.VMEM((nfsdp,) + piece, bf16),
                pltpu.SemaphoreType.DMA((12,)),
                pltpu.SemaphoreType.DMA((4,)),
            ],
            name="heads",
        )(pos, cols, counts, feats, *near, *far, w0, wup, wdn, wfar_up, wfar_dn, cotans[j])
        outs.append(lax.all_to_all(out.reshape(nclus, rows, HD), "clus", 0, 0, tiled=True))
        far_a = shift(g3, [(0, 3)])
        far_b = shift(g1, [(3, 0)])
        up1 = shift(g2, [(0, 1), (1, 2)])
        dn1 = shift(g2, [(3, 2), (2, 1)])
        up2 = shift(add(g1, up1), [(0, 1), (1, 2), (2, 3)])
        dn2 = shift(add(g3, dn1), [(3, 2), (2, 1), (1, 0)])
        total = add(g0, up2, dn2, far_a, far_b)
        grads.append(lax.all_to_all(total, "clus", 0, 0, tiled=True))
    out = pl.pallas_call(
        merge_heads,
        in_specs=[VMEM] * slots,
        out_specs=VMEM,
        out_shape=shape((rows, half)),
        name="merge_out",
    )(*outs)
    gq, gkv = pl.pallas_call(
        merge_grads,
        in_specs=[VMEM] * slots,
        out_specs=[VMEM] * 2,
        out_shape=[shape((wrows, half), jnp.float32)] * 2,
        name="merge_grads",
    )(*grads)
    return out, gq, gkv


def add(*xs):
    total = xs[0].astype(jnp.float32)
    for x in xs[1:]:
        total = total + x.astype(jnp.float32)
    return total.astype(jnp.bfloat16)


def on_device(feats, w_query, w_keyval, grad_out, col_block, col_count):
    rows = feats.shape[0]
    half = w_query.shape[1]
    nlocal = rows // BLK
    heads_here = half // HD
    nclus = lax.axis_size("clus")
    nfsdp = lax.axis_size("fsdp")
    clus_at = lax.axis_index("clus")
    fsdp_at = lax.axis_index("fsdp")
    myself = clus_at * nfsdp + fsdp_at
    scale = 1.0 / math.sqrt(HD)
    columns = feats
    acc_query = jnp.dot(
        columns,
        lax.all_gather(w_query.astype(jnp.bfloat16), ("clus", "fsdp"), axis=0, tiled=True),
        preferred_element_type=jnp.float32,
    )
    acc_keyval = jnp.dot(
        columns,
        lax.all_gather(w_keyval.astype(jnp.bfloat16), ("clus", "fsdp"), axis=0, tiled=True),
        preferred_element_type=jnp.float32,
    )
    query = acc_query.astype(jnp.bfloat16)
    keyval = acc_keyval.astype(jnp.bfloat16)
    all_cols = col_block.reshape(nclus, nfsdp, nlocal, NCOL)
    all_counts = col_count.reshape(nclus, nfsdp, nlocal)
    peer_cols = lax.dynamic_index_in_dim(all_cols, fsdp_at, 1, keepdims=False)
    peer_counts = lax.dynamic_index_in_dim(all_counts, fsdp_at, 1, keepdims=False)
    peer_live = jnp.arange(NCOL, dtype=jnp.int32)[None, None, :] < peer_counts[:, :, None]
    my_blocks = myself * nlocal + jnp.arange(nlocal, dtype=jnp.int32)
    listed = (peer_cols[:, :, :, None] == my_blocks[None, None, None, :]) & peer_live[:, :, :, None]
    needed = jnp.any(listed, axis=(1, 2)) & (jnp.arange(nclus, dtype=jnp.int32) != clus_at)[:, None]
    flat_keyval = keyval.reshape(nlocal, BLK * half)
    outgoing = jnp.dot(needed.astype(jnp.bfloat16), flat_keyval, preferred_element_type=jnp.float32)
    outgoing = outgoing.astype(jnp.bfloat16).reshape(nclus, BLK, half)
    received = lax.all_to_all(outgoing, "clus", split_axis=0, concat_axis=0, tiled=True)
    my_cols = lax.dynamic_slice_in_dim(col_block, myself * nlocal, nlocal, 0)
    my_counts = lax.dynamic_slice_in_dim(col_count, myself * nlocal, nlocal, 0)
    col_cluster = my_cols // nlocal
    inside = col_cluster == myself
    table_index = jnp.where(inside, my_cols % nlocal, nlocal + col_cluster // nfsdp).reshape(-1)
    table = jnp.concatenate([keyval.reshape(nlocal, BLK, half), received], 0)
    keys = jnp.take(table, table_index, axis=0).reshape(nlocal, NCOL * BLK, heads_here, HD)
    queries = query.reshape(nlocal, BLK, heads_here, HD)
    cotans = grad_out.reshape(nlocal, BLK, heads_here, HD)
    valid = jnp.repeat(jnp.arange(NCOL, dtype=jnp.int32)[None, :] < my_counts[:, None], BLK, axis=1)
    score = jnp.einsum("bqhd,bkhd->bhqk", queries, keys, preferred_element_type=jnp.float32) * scale
    score = jnp.where(valid[:, None, None, :], score, -1e30)
    top = jnp.max(score, axis=-1, keepdims=True)
    expo = jnp.exp(score - top)
    prob = expo / jnp.sum(expo, axis=-1, keepdims=True)
    prob_b = prob.astype(jnp.bfloat16)
    out = (
        jnp.einsum("bhqk,bkhd->bqhd", prob_b, keys, preferred_element_type=jnp.float32)
        .astype(jnp.bfloat16)
        .reshape(rows, half)
    )
    dprob = jnp.einsum("bqhd,bkhd->bhqk", cotans, keys, preferred_element_type=jnp.float32)
    delta = jnp.sum(prob * dprob, axis=-1, keepdims=True)
    dscore = (prob * (dprob - delta)).astype(jnp.bfloat16)
    dquery = (
        (jnp.einsum("bhqk,bkhd->bqhd", dscore, keys, preferred_element_type=jnp.float32) * scale)
        .astype(jnp.bfloat16)
        .reshape(rows, half)
    )
    dkeys = (
        jnp.einsum("bhqk,bqhd->bkhd", dscore, queries, preferred_element_type=jnp.float32) * scale
    )
    dkeys = dkeys + jnp.einsum(
        "bhqk,bqhd->bkhd", prob_b, cotans, preferred_element_type=jnp.float32
    )
    dkeys = dkeys.reshape(nlocal * NCOL, BLK * half)
    onehot = (table_index[:, None] == jnp.arange(nlocal + nclus, dtype=jnp.int32)[None, :]).astype(
        jnp.float32
    )
    grad_table = jnp.dot(onehot.T, dkeys, precision=lax.Precision.HIGHEST)
    returned = lax.all_to_all(
        grad_table[nlocal:].reshape(nclus, BLK, half),
        "clus",
        split_axis=0,
        concat_axis=0,
        tiled=True,
    )
    dkeyval = grad_table[:nlocal] + jnp.dot(
        needed.T.astype(jnp.float32),
        returned.reshape(nclus, BLK * half),
        precision=lax.Precision.HIGHEST,
    )
    dkeyval = dkeyval.astype(jnp.bfloat16).reshape(rows, half)
    both_grads = jnp.concatenate([dquery, dkeyval], 1)
    columns = feats
    partial_sum = lax.psum_scatter(
        lax.dot_general(
            columns, both_grads, (((0,), (0,)), ((), ())), preferred_element_type=jnp.float32
        ).astype(jnp.bfloat16),
        "clus",
        scatter_dimension=0,
        tiled=True,
    ).astype(jnp.float32)
    final = lax.psum_scatter(partial_sum, "fsdp", scatter_dimension=0, tiled=True)
    return (out, final[:, :half], final[:, half:])


def solution(mesh):
    square = mesh.shape["clus"] == 4 and mesh.shape["fsdp"] == 4 and mesh.shape["head"] == 2
    return jax.shard_map(
        in_plane if square else on_device,
        mesh=mesh,
        in_specs=(
            P(("clus", "fsdp"), None),
            P(("clus", "fsdp"), "head"),
            P(("clus", "fsdp"), "head"),
            P(("clus", "fsdp"), "head"),
            P(),
            P(),
        ),
        out_specs=(
            P(("clus", "fsdp"), "head"),
            P(("clus", "fsdp"), "head"),
            P(("clus", "fsdp"), "head"),
        ),
        check_vma=False,
    )
```
